32 devices in a mesh: tok: 16 (over z, y, x), tp: 2 (over core).
Axes of the slice: x: 2, y: 2, z: 4, core: 2. Of those that a mesh axis runs over, the one named last changes fastest.
Arguments:
- tokens: bfloat16 [6144, 1024], P('tok'), may hold values from -6 to 6
- cotangent: bfloat16 [6144, 1024], P('tok'), may hold values from -6 to 6
- image_ids: int32 [6144], P('tok'), may hold values from 0 to 5, never falling along the last dimension, each value on 1 to 1370 neighbouring positions
- w_qkv: bfloat16 [2, 1024, 3, 1024], P(None, 'tok', None, 'tp'), may hold values from -1 to 1
- w_out: bfloat16 [2, 1024, 1024], P(None, 'tok', 'tp'), may hold values from -1.5 to 1.5
- w_up: bfloat16 [2, 1024, 4096], P(None, 'tok', 'tp'), may hold values from -0.1875 to 0.1875
- w_down: bfloat16 [2, 1024, 4096], P(None, 'tok', 'tp'), may hold values from -0.09375 to 0.09375
- vectors: bfloat16 [2, 14, 1024], P(None, None, 'tok'), may hold values from -2 to 2
Outputs:
- outputs: float32 [6144, 1024], P('tok')
- grad_tokens: float32 [6144, 1024], P('tok')
- grad_qkv: float32 [2, 1024, 3, 1024], P(None, 'tok', None, 'tp')
- grad_out: float32 [2, 1024, 1024], P(None, 'tok', 'tp')
- grad_up: float32 [2, 1024, 4096], P(None, 'tok', 'tp')
- grad_down: float32 [2, 1024, 4096], P(None, 'tok', 'tp')
- grad_vectors: float32 [2, 14, 1024], P(None, None, ('tok', 'tp'))
The draws below stay inside these ranges and needn't reach their ends.
Inputs may be any that keep to these rules, and one draw needn't show every extreme that they name: `image_ids`: image ids never fall along the tokens, every id from 0 to 5 is used, each image holds 1 to 1370 tokens and one holds exactly 1370.
All inputs are finite; a program needn't handle non-finite values.
Results may differ from the reference program's by a relative error of at most 0.04.
Values may be sent and summed in bfloat16 or wider, within the bound.
No kernel may reach another device: no remote copies, remote signals or barrier semaphores. Data moves between devices by JAX's collectives and lax.ppermute only.
A program may use at most 256 MiB of HBM per device.

```python
import math
import jax
import jax.numpy as jnp
import numpy as np
from jax import lax

D = 1024
FF = 4096
HEAD = 64
IMG_LEN = 1370
LAYERS = 2
TOK_DEV = 384
HEADS = 16
TOKENS = 6144
IMAGES = 6
REACH = 4
VROWS = 14
N_TOK = 16


def draw_tokens(key, part):
    base_key = jax.random.fold_in(key, 3)
    value_rows = jnp.clip(jax.random.normal(base_key, (TOKENS, D), jnp.float32), -6.0, 6.0)
    return value_rows.astype(jnp.bfloat16)


def draw_w_qkv(key, part):
    base_key = jax.random.fold_in(key, 13)
    value_rows = jnp.clip(jax.random.normal(base_key, (LAYERS, D, 3, D), jnp.float32), -4.0, 4.0) * D ** (-0.5)
    return value_rows.astype(jnp.bfloat16)


def draw_vectors(key, part):
    noise_key = jax.random.fold_in(key, 7)
    noise = jnp.clip(jax.random.normal(noise_key, (LAYERS, VROWS, D), jnp.float32), -2.0, 2.0)
    rows = jnp.arange(VROWS)
    gains = (rows == 0) | (rows == 6)
    scales = (rows == 5) | (rows == 9)
    centre = jnp.where(gains, 1.0, jnp.where(scales, 0.8, 0.0))
    spread = jnp.where(gains, 0.25, jnp.where(scales, 0.3, 0.5))
    return (centre[None, :, None] + spread[None, :, None] * noise).astype(jnp.bfloat16)


def shard_levels(stream_key, dims, shards, smallest, high):
    loudness, own = 1.0, jax.random.fold_in(stream_key, 6)
    for position, shards_of in shards:
        heights = jnp.exp(jax.random.uniform(jax.random.fold_in(own, position), (shards_of,), jnp.float32, smallest / len(shards), high / len(shards)))
        loudness = loudness * jnp.repeat(heights, dims[position] // shards_of).reshape([-1 if axis == position else 1 for axis in range(len(dims))])
    return loudness


def length_profile(number_of, total, bound, lean):
    weights = [(1 << 20) // math.isqrt(standing ** lean) + 1 for standing in range(2, number_of + 1)]
    surplus, given = total - bound - (number_of - 1), [1] * (number_of - 1)
    while surplus > 0:
        candidates = [i for i in range(number_of - 1) if given[i] < bound]
        mass, remaining = sum([weights[i] for i in candidates]), surplus
        for i in candidates:
            extra = min(bound - given[i], max(1, remaining * weights[i] // mass), surplus)
            given[i] = given[i] + extra
            surplus = surplus - extra
    return np.array([bound] + given)


def uneven(own_key, amount, total, limit, slope):
    if amount == 2:
        one = jax.random.randint(own_key, (), max(1, total - limit), min(limit, total - 1) + 1)
        return jnp.stack([one, total - one])
    sizes = jnp.asarray(length_profile(amount, total, limit, slope), jnp.int32)
    couples = (amount - 1) // 2
    donor, receiver = sizes[1:1 + 2 * couples:2], sizes[2:2 + 2 * couples:2]
    margin = jnp.minimum(donor - 1, limit - receiver)
    shifted = jax.random.randint(jax.random.fold_in(own_key, 1), (couples,), 0, 1 << 20) % (margin + 1)
    sizes = sizes.at[1:1 + 2 * couples:2].set(donor - shifted).at[2:2 + 2 * couples:2].set(receiver + shifted)
    return sizes[jax.random.permutation(jax.random.fold_in(own_key, 2), amount)]


def gaussian(stream_key, dims, deviation, most, split=(), kind=jnp.bfloat16):
    values = deviation * jax.random.normal(stream_key, dims, jnp.float32)
    if split:
        values = values * shard_levels(stream_key, dims, split, -0.22, 0.18)
    return jnp.clip(values, -most, most).astype(kind)


def setup_inputs(seed: int = 0) -> dict:
    splits = jax.random.split(jax.random.key(seed), 9)
    return {
        "tokens": draw_tokens(jax.random.fold_in(splits[8], 71), 0),
        "cotangent": gaussian(splits[1], (TOKENS, D), 1.0, 6.0, ((0, 16),)),
        "image_ids": jnp.searchsorted(jnp.cumsum(uneven(splits[2], IMAGES, TOKENS, IMG_LEN, 0)), jnp.arange(TOKENS), side="right").astype(jnp.int32),
        "w_qkv": draw_w_qkv(jax.random.fold_in(splits[8], 71), 0),
        "w_out": gaussian(splits[4], (LAYERS, D, D), (D // 64) ** -0.5, 1.5, ((1, 16), (2, 2))),
        "w_up": gaussian(splits[5], (LAYERS, D, FF), D ** -0.5, 0.1875, ((1, 16), (2, 2))),
        "w_down": gaussian(splits[6], (LAYERS, D, FF), FF ** -0.5, 0.09375, ((1, 16), (2, 2))),
        "vectors": draw_vectors(jax.random.fold_in(splits[8], 71), 0),
    }


EPS = 1e-06
NEG = -1e+30
ROOT_HALF = 0.7071067811865476
INV_ROOT_TWO_PI = 0.3989422804014327

def rounded(value):
    return lax.optimization_barrier(value.astype(jnp.bfloat16))

def layer_norm_forward(x, norm_gain, norm_shift):
    token_mean = lax.optimization_barrier(jnp.mean(x, axis=-1, keepdims=True))
    centered_input = x - token_mean
    inverse_deviation = lax.rsqrt(lax.optimization_barrier(jnp.mean(centered_input * centered_input, axis=-1, keepdims=True)) + EPS)
    standardized_input = centered_input * inverse_deviation
    return (standardized_input, inverse_deviation, standardized_input * norm_gain + norm_shift)

def layer_norm_backward(normed_output_gradient, standardized_input, inverse_deviation, norm_gain):
    standardized_gradient = normed_output_gradient * norm_gain
    inner_activation = standardized_gradient - lax.optimization_barrier(jnp.mean(standardized_gradient, axis=-1, keepdims=True))
    return inverse_deviation * (inner_activation - standardized_input * lax.optimization_barrier(jnp.mean(standardized_gradient * standardized_input, axis=-1, keepdims=True)))

def gelu_pair(pre):
    cumul = 0.5 * (1.0 + jax.scipy.special.erf(pre * ROOT_HALF))
    return (pre * cumul, cumul + pre * INV_ROOT_TWO_PI * jnp.exp(-0.5 * pre * pre))

def padded_inputs(key_rows, value_rows, image_ids):
    span = REACH * TOK_DEV
    keys_pad = jnp.pad(key_rows, ((span, span), (0, 0), (0, 0)))
    values_pad = jnp.pad(value_rows, ((span, span), (0, 0), (0, 0)))
    ids_pad = jnp.pad(image_ids, (span, span), constant_values=-1)
    return (keys_pad, values_pad, ids_pad)

def block_scores(query_rows, keys_pad, ids_pad, image_ids, start, scale):
    window = (2 * REACH + 1) * TOK_DEV
    q_blk = lax.dynamic_slice_in_dim(query_rows, start, TOK_DEV, 0).astype(jnp.float32)
    k_win = lax.dynamic_slice_in_dim(keys_pad, start, window, 0).astype(jnp.float32)
    id_q = lax.dynamic_slice_in_dim(image_ids, start, TOK_DEV, 0)
    id_w = lax.dynamic_slice_in_dim(ids_pad, start, window, 0)
    allowed = id_q[:, None] == id_w[None, :]
    scores = jnp.einsum('qhd,khd->hqk', q_blk, k_win) * scale
    return (q_blk, k_win, jnp.where(allowed[None], scores, NEG))

def attend_forward(query_rows, key_rows, value_rows, image_ids, scale):
    window = (2 * REACH + 1) * TOK_DEV
    keys_pad, values_pad, ids_pad = padded_inputs(key_rows, value_rows, image_ids)

    def block(index):
        start = (index * TOK_DEV).astype(jnp.int32)
        q_blk, k_win, scores = block_scores(query_rows, keys_pad, ids_pad, image_ids, start, scale)
        v_win = lax.dynamic_slice_in_dim(values_pad, start, window, 0).astype(jnp.float32)
        top = lax.optimization_barrier(jnp.max(scores, axis=-1, keepdims=True))
        expd = jnp.exp(scores - top)
        total = lax.optimization_barrier(jnp.sum(expd, axis=-1, keepdims=True))
        prob = rounded(expd / total).astype(jnp.float32)
        merged = jnp.einsum('hqk,khd->qhd', prob, v_win).astype(jnp.bfloat16)
        return (merged, top[:, :, 0] + jnp.log(total[:, :, 0]))
    merged, log_sum_exponent = lax.map(block, jnp.arange(N_TOK, dtype=jnp.int32))
    return (merged.reshape(TOKENS, HEADS, HEAD), log_sum_exponent)

def attend_backward(query_rows, key_rows, value_rows, image_ids, log_sum_exponent, grad_att, scale):
    span = REACH * TOK_DEV
    window = (2 * REACH + 1) * TOK_DEV
    keys_pad, values_pad, ids_pad = padded_inputs(key_rows, value_rows, image_ids)
    zeros = jnp.zeros((TOKENS + 2 * span, HEADS, HEAD), jnp.float32)

    def block(carry, inputs):
        acc_k, acc_v = carry
        index, lse_blk = inputs
        start = (index * TOK_DEV).astype(jnp.int32)
        q_blk, k_win, scores = block_scores(query_rows, keys_pad, ids_pad, image_ids, start, scale)
        v_win = lax.dynamic_slice_in_dim(values_pad, start, window, 0).astype(jnp.float32)
        g_blk = lax.dynamic_slice_in_dim(grad_att, start, TOK_DEV, 0).astype(jnp.float32)
        prob = jnp.exp(scores - lse_blk[:, :, None])
        prob_low = rounded(prob).astype(jnp.float32)
        grad_v = jnp.einsum('hqk,qhd->khd', prob_low, g_blk)
        grad_p = jnp.einsum('qhd,khd->hqk', g_blk, v_win)
        delta = lax.optimization_barrier(jnp.sum(prob * grad_p, axis=-1, keepdims=True))
        grad_s = rounded(prob * (grad_p - delta) * scale).astype(jnp.float32)
        grad_q = jnp.einsum('hqk,khd->qhd', grad_s, k_win)
        grad_k = jnp.einsum('hqk,qhd->khd', grad_s, q_blk)
        acc_k = lax.dynamic_update_slice_in_dim(acc_k, lax.dynamic_slice_in_dim(acc_k, start, window, 0) + grad_k, start, 0)
        acc_v = lax.dynamic_update_slice_in_dim(acc_v, lax.dynamic_slice_in_dim(acc_v, start, window, 0) + grad_v, start, 0)
        return ((acc_k, acc_v), grad_q)
    (acc_k, acc_v), grad_q = lax.scan(block, (zeros, zeros), (jnp.arange(N_TOK, dtype=jnp.int32), log_sum_exponent))
    return (grad_q.reshape(TOKENS, HEADS, HEAD), acc_k[span:span + TOKENS], acc_v[span:span + TOKENS])

def reference(tokens, cotangent, image_ids, w_qkv, w_out, w_up, w_down, vectors):
    scale = 1.0 / math.sqrt(HEAD)
    residual_state = tokens.astype(jnp.float32)
    saved_residuals = []
    for encoder_layer in range(LAYERS):
        vector_parameters = vectors[encoder_layer].astype(jnp.float32)
        first_standardized, first_inverse_deviation, first_normed_input = layer_norm_forward(residual_state, vector_parameters[0], vector_parameters[1])
        first_hidden_state = rounded(first_normed_input)
        mixed = jnp.dot(first_hidden_state, w_qkv[encoder_layer].reshape(D, 3 * D), preferred_element_type=jnp.float32).reshape(TOKENS, 3, D)
        query_rows = rounded(mixed[:, 0] + vector_parameters[2]).reshape(TOKENS, HEADS, HEAD)
        key_rows = rounded(mixed[:, 1]).reshape(TOKENS, HEADS, HEAD)
        value_rows = rounded(mixed[:, 2] + vector_parameters[3]).reshape(TOKENS, HEADS, HEAD)
        merged, log_sum_exponent = attend_forward(query_rows, key_rows, value_rows, image_ids, scale)
        attention_output = merged.reshape(TOKENS, D)
        attention_branch = jnp.dot(attention_output, w_out[encoder_layer].T, preferred_element_type=jnp.float32) + vector_parameters[4]
        middle_state = residual_state + vector_parameters[5] * attention_branch
        second_standardized, second_inverse_deviation, second_normed_input = layer_norm_forward(middle_state, vector_parameters[6], vector_parameters[7])
        second_hidden_state = rounded(second_normed_input)
        pre = jnp.dot(second_hidden_state, w_up[encoder_layer], preferred_element_type=jnp.float32) + vector_parameters[10:].reshape(FF)
        act, gelu_slope = gelu_pair(pre)
        hidden_activation = rounded(act)
        feedforward_branch = jnp.dot(hidden_activation, w_down[encoder_layer].T, preferred_element_type=jnp.float32) + vector_parameters[8]
        saved_residuals.append((residual_state, first_standardized, first_inverse_deviation, first_hidden_state, query_rows, key_rows, value_rows, log_sum_exponent, attention_output, attention_branch, second_standardized, second_inverse_deviation, second_hidden_state, gelu_slope, hidden_activation, feedforward_branch))
        residual_state = middle_state + vector_parameters[9] * feedforward_branch
    outputs = residual_state
    upstream_gradient = cotangent.astype(jnp.float32)
    grads_qkv = [None] * LAYERS
    grads_out = [None] * LAYERS
    grads_up = [None] * LAYERS
    grads_down = [None] * LAYERS
    grads_vec = [None] * LAYERS
    for encoder_layer in reversed(range(LAYERS)):
        vector_parameters = vectors[encoder_layer].astype(jnp.float32)
        residual_state, first_standardized, first_inverse_deviation, first_hidden_state, query_rows, key_rows, value_rows, log_sum_exponent, attention_output, attention_branch, second_standardized, second_inverse_deviation, second_hidden_state, gelu_slope, hidden_activation, feedforward_branch = saved_residuals[encoder_layer]
        grad_ls2 = lax.optimization_barrier(jnp.sum(upstream_gradient * feedforward_branch, axis=0))
        grad_branch2 = vector_parameters[9] * upstream_gradient
        grad_b2 = lax.optimization_barrier(jnp.sum(grad_branch2, axis=0))
        low_b2 = rounded(grad_branch2)
        grads_down[encoder_layer] = jnp.dot(low_b2.T, hidden_activation, preferred_element_type=jnp.float32)
        grad_pre = jnp.dot(low_b2, w_down[encoder_layer], preferred_element_type=jnp.float32) * gelu_slope
        grad_bias_up = lax.optimization_barrier(jnp.sum(grad_pre, axis=0))
        low_pre = rounded(grad_pre)
        grads_up[encoder_layer] = jnp.dot(second_hidden_state.T, low_pre, preferred_element_type=jnp.float32)
        second_normed_gradient = jnp.dot(low_pre, w_up[encoder_layer].T, preferred_element_type=jnp.float32)
        second_gain_gradient = lax.optimization_barrier(jnp.sum(second_normed_gradient * second_standardized, axis=0))
        grad_c2 = lax.optimization_barrier(jnp.sum(second_normed_gradient, axis=0))
        middle_gradient = upstream_gradient + layer_norm_backward(second_normed_gradient, second_standardized, second_inverse_deviation, vector_parameters[6])
        grad_ls1 = lax.optimization_barrier(jnp.sum(middle_gradient * attention_branch, axis=0))
        grad_branch1 = vector_parameters[5] * middle_gradient
        grad_bo = lax.optimization_barrier(jnp.sum(grad_branch1, axis=0))
        low_b1 = rounded(grad_branch1)
        grads_out[encoder_layer] = jnp.dot(low_b1.T, attention_output, preferred_element_type=jnp.float32)
        grad_att = rounded(jnp.dot(low_b1, w_out[encoder_layer], preferred_element_type=jnp.float32)).reshape(TOKENS, HEADS, HEAD)
        grad_q, grad_k, grad_v = attend_backward(query_rows, key_rows, value_rows, image_ids, log_sum_exponent, grad_att, scale)
        grad_q = grad_q.reshape(TOKENS, D)
        grad_k = grad_k.reshape(TOKENS, D)
        grad_v = grad_v.reshape(TOKENS, D)
        grad_bq = lax.optimization_barrier(jnp.sum(grad_q, axis=0))
        grad_bv = lax.optimization_barrier(jnp.sum(grad_v, axis=0))
        low_qkv = rounded(jnp.stack([grad_q, grad_k, grad_v], axis=1).reshape(TOKENS, 3 * D))
        grads_qkv[encoder_layer] = jnp.dot(first_hidden_state.T, low_qkv, preferred_element_type=jnp.float32).reshape(D, 3, D)
        first_normed_gradient = jnp.dot(low_qkv, w_qkv[encoder_layer].reshape(D, 3 * D).T, preferred_element_type=jnp.float32)
        first_gain_gradient = lax.optimization_barrier(jnp.sum(first_normed_gradient * first_standardized, axis=0))
        grad_c1 = lax.optimization_barrier(jnp.sum(first_normed_gradient, axis=0))
        upstream_gradient = middle_gradient + layer_norm_backward(first_normed_gradient, first_standardized, first_inverse_deviation, vector_parameters[0])
        small = jnp.stack([first_gain_gradient, grad_c1, grad_bq, grad_bv, grad_bo, grad_ls1, second_gain_gradient, grad_c2, grad_b2, grad_ls2])
        grads_vec[encoder_layer] = jnp.concatenate([small, grad_bias_up.reshape(FF // D, D)], axis=0)
    return (outputs, upstream_gradient, jnp.stack(grads_qkv), jnp.stack(grads_out), jnp.stack(grads_up), jnp.stack(grads_down), jnp.stack(grads_vec))
```

```python
import functools
import math

import jax
import jax.numpy as jnp
from jax import lax
from jax.experimental import pallas as pl
from jax.experimental.pallas import tpu as pltpu
from jax.sharding import PartitionSpec as P

HEAD = 64
REACH = 4
EPS = 1e-06
NEG = -1e30
ROOT_HALF = 0.7071067811865476
INV_ROOT_TWO_PI = 0.3989422804014327
BF = jnp.bfloat16
F32 = jnp.float32


def swap_tok(x, mask):
    count = lax.axis_size("tok")
    return lax.ppermute(x, "tok", [(i, i ^ mask) for i in range(count)])


def swap_core(x, mask0, mask1):
    count, parts = lax.axis_size("tok"), lax.axis_size("tp")
    pairs = [
        (t * parts + c, (t ^ (mask1 if c % 2 else mask0)) * parts + c)
        for t in range(count)
        for c in range(parts)
    ]
    return lax.ppermute(x, ("tok", "tp"), pairs)


def shift_tok(x, by):
    count = lax.axis_size("tok")
    return lax.ppermute(x, "tok", [(i, i + by) for i in range(count) if 0 <= i + by < count])


def swap_tp(x):
    return lax.ppermute(x, "tp", [(0, 1), (1, 0)])


def over_tp(value):
    own = lax.optimization_barrier(value.astype(BF))
    return own.astype(F32) + swap_tp(own).astype(F32)


def gather_rows(x):
    return lax.all_gather(x, "tok", axis=0, tiled=True)


def scatter_rows(x):
    return lax.psum_scatter(x, "tok", scatter_dimension=0, tiled=True)


def scatter_small(x):
    count = lax.axis_size("tok")
    upper = count // REACH
    me = lax.axis_index("tok")
    x = jnp.take(x, jnp.arange(count) ^ me, axis=0).reshape(upper, REACH, -1)
    d0, d1, d2, d3 = (x[:, q] for q in range(REACH))
    send = lax.optimization_barrier(d3.astype(BF))
    d2 = d2 + swap_tok(send, 1).astype(F32)
    d0 = d0 + swap_tok(lax.optimization_barrier(d1.astype(BF)), 1).astype(F32)
    d0 = d0 + swap_tok(lax.optimization_barrier(d2.astype(BF)), 2).astype(F32)
    low = lax.optimization_barrier(d0.astype(BF))
    total = d0[0]
    for j in range(1, upper):
        total = total + swap_tok(low[j], REACH * j).astype(F32)
    return total


def relative(parts, place):
    out = []
    for j in range(REACH):
        value = parts[j ^ 3]
        for k in (2, 1, 0):
            value = jnp.where(place == k, parts[j ^ k], value)
        out.append(value)
    return out


def _stack_heads(x, heads):
    lane = lax.broadcasted_iota(jnp.int32, x.shape, 1) // HEAD
    return jnp.concatenate([jnp.where(lane == h, x, jnp.zeros_like(x)) for h in range(heads)], axis=0)


def _unstack(t, heads, width):
    rows = [t[h * HEAD : (h + 1) * HEAD, h * width : (h + 1) * width] for h in range(heads)]
    return jnp.concatenate(rows, axis=0).T


def _nt(a, b):
    return lax.dot_general(a, b, (((1,), (1,)), ((), ())), preferred_element_type=F32)


def _nn(a, b):
    return jnp.dot(a, b, preferred_element_type=F32)


def attend_kernel(heads, scale, qlo, qhi, klo, khi, q_ref, kv0, kv1, kv2, qid_ref, kid_ref,
                  o_ref, lse_ref, k_s, vt_s, acc_s, m_s, l_s):
    tq, feats = q_ref.shape
    tk = tq
    seg = kv0.shape[0] // tk
    nk = 3 * seg
    step = pl.program_id(0)

    @pl.when(step == 0)
    def _():
        for s, ref in enumerate((kv0, kv1, kv2)):
            for b in range(seg):
                at = (s * seg + b) * tk
                k_s[at : at + tk, :] = ref[b * tk : (b + 1) * tk, :feats]
                vt_s[s * seg + b] = ref[b * tk : (b + 1) * tk, feats:].astype(F32).T.astype(BF)

    q = _stack_heads(q_ref[...] * jnp.asarray(scale, BF), heads)
    qid = jnp.concatenate([qid_ref[0]] * heads, axis=1)
    m_s[...] = jnp.full_like(m_s, NEG)
    l_s[...] = jnp.zeros_like(l_s)
    acc_s[...] = jnp.zeros_like(acc_s)
    lo, hi = qlo[step], qhi[step]

    def tile(t, carry):
        @pl.when((klo[t] <= hi) & (khi[t] >= lo))
        def _():
            at = pl.multiple_of(t * tk, tk)
            s = _nt(k_s[pl.ds(at, tk), :], q)
            s = jnp.where(kid_ref[pl.ds(at, tk), :] == qid, s, NEG)
            old = m_s[...]
            new = jnp.maximum(old, jnp.max(s, axis=0, keepdims=True))
            e = jnp.exp(s - new)
            keep = jnp.exp(old - new)
            m_s[...] = new
            l_s[...] = l_s[...] * keep + jnp.sum(e, axis=0, keepdims=True)
            acc_s[...] = acc_s[...] * keep + _nn(vt_s[t], e.astype(BF))
        return carry

    lax.fori_loop(0, nk, tile, 0)
    total = l_s[...]
    o_ref[...] = _unstack(acc_s[...] / total, heads, tq).astype(BF)
    lse_ref[0] = m_s[...] + jnp.log(total)


def attend_back_kernel(heads, scale, qlo, qhi, klo, khi, q_ref, o_ref, g_ref, lse_ref, kv0, kv1, kv2,
                       qid_ref, kid_ref, dq_ref, d0_ref, d1_ref, d2_ref,
                       k_s, v_s, kt_s, dk_s, dv_s, acc_s):
    tq, feats = q_ref.shape
    tk = tq
    seg = kv0.shape[0] // tk
    nk = 3 * seg
    step = pl.program_id(0)

    @pl.when(step == 0)
    def _():
        for s, ref in enumerate((kv0, kv1, kv2)):
            for b in range(seg):
                at = (s * seg + b) * tk
                k = ref[b * tk : (b + 1) * tk, :feats]
                k_s[at : at + tk, :] = k
                v_s[at : at + tk, :] = ref[b * tk : (b + 1) * tk, feats:]
                kt_s[s * seg + b] = k.astype(F32).T.astype(BF)
        dk_s[...] = jnp.zeros_like(dk_s)
        dv_s[...] = jnp.zeros_like(dv_s)

    q = _stack_heads(q_ref[...] * jnp.asarray(scale, BF), heads)
    g = _stack_heads(g_ref[...], heads)
    prod = (o_ref[...].astype(F32) * g_ref[...].astype(F32)).T
    delta = jnp.concatenate(
        [jnp.sum(prod[h * HEAD : (h + 1) * HEAD], axis=0, keepdims=True) for h in range(heads)], axis=1
    )
    lse = lse_ref[0]
    qid = jnp.concatenate([qid_ref[0]] * heads, axis=1)
    acc_s[...] = jnp.zeros_like(acc_s)
    lo, hi = qlo[step], qhi[step]

    def tile(t, carry):
        @pl.when((klo[t] <= hi) & (khi[t] >= lo))
        def _():
            at = pl.multiple_of(t * tk, tk)
            rows = pl.ds(at, tk)
            s = _nt(k_s[rows, :], q)
            prob = jnp.exp(jnp.where(kid_ref[rows, :] == qid, s - lse, NEG))
            dv_s[rows, :] += _nn(prob.astype(BF), g)
            dp = _nt(v_s[rows, :], g)
            ds = (prob * (dp - delta)).astype(BF)
            dk_s[rows, :] += _nn(ds, q)
            acc_s[...] += _nn(kt_s[t], ds)
        return carry

    lax.fori_loop(0, nk, tile, 0)
    dq_ref[...] = (_unstack(acc_s[...], heads, tq) * scale).astype(BF)

    @pl.when(step == pl.num_programs(0) - 1)
    def _():
        for s, ref in enumerate((d0_ref, d1_ref, d2_ref)):
            at = s * seg * tk
            ref[:, :feats] = dk_s[at : at + seg * tk, :].astype(ref.dtype)
            ref[:, feats:] = dv_s[at : at + seg * tk, :].astype(ref.dtype)


class Attention:
    def __init__(self, ids, rows, feats):
        self.rows, self.feats, self.heads = rows, feats, feats // HEAD
        self.scale = 1.0 / math.sqrt(HEAD)
        self.lo, self.hi = ids[:, 0], ids[:, -1]
        own = ids[REACH : 2 * REACH]
        self.qlo, self.qhi = own[:, 0], own[:, -1]
        self.qid = own.reshape(REACH, 1, rows)
        self.kid = ids.reshape(-1, 1)

    def specs(self):
        rows, feats = self.rows, self.feats
        tile = pl.BlockSpec((rows, feats), lambda i, *_: (i, 0))
        keys = pl.BlockSpec((REACH * rows, 2 * feats), lambda i, *_: (0, 0), pipeline_mode=pl.Buffered(1))
        qid = pl.BlockSpec((1, 1, rows), lambda i, *_: (i, 0, 0))
        kid = pl.BlockSpec((3 * REACH * rows, 1), lambda i, *_: (0, 0), pipeline_mode=pl.Buffered(1))
        lse = pl.BlockSpec((1, 1, self.heads * rows), lambda i, *_: (i, 0, 0))
        return tile, keys, qid, kid, lse

    def cost(self, products):
        pairs = REACH * self.rows * 4 * self.rows * self.heads
        return pl.CostEstimate(
            flops=2 * products * pairs * self.feats, transcendentals=pairs,
            bytes_accessed=16 * REACH * self.rows * self.feats,
        )

    def forward(self, q, keys):
        tile, kspec, qid, kid, lse = self.specs()
        rows, feats, heads = self.rows, self.feats, self.heads
        width, count = heads * rows, 3 * REACH
        return pl.pallas_call(
            functools.partial(attend_kernel, heads, self.scale),
            name="attend",
            out_shape=(
                jax.ShapeDtypeStruct((REACH * rows, feats), BF),
                jax.ShapeDtypeStruct((REACH, 1, width), F32),
            ),
            grid_spec=pltpu.PrefetchScalarGridSpec(
                num_scalar_prefetch=4, grid=(REACH,),
                in_specs=[tile, kspec, kspec, kspec, qid, kid],
                out_specs=[tile, lse],
                scratch_shapes=[
                    pltpu.VMEM((count * rows, feats), BF),
                    pltpu.VMEM((count, feats, rows), BF),
                    pltpu.VMEM((feats, width), F32),
                    pltpu.VMEM((1, width), F32),
                    pltpu.VMEM((1, width), F32),
                ],
            ),
            cost_estimate=self.cost(2),
        )(self.qlo, self.qhi, self.lo, self.hi, q, *keys, self.qid, self.kid)

    def backward(self, q, keys, out, lse_value, grad):
        tile, kspec, qid, kid, lse = self.specs()
        rows, feats, heads = self.rows, self.feats, self.heads
        width, count = heads * rows, 3 * REACH
        whole = pl.BlockSpec((REACH * rows, 2 * feats), lambda i, *_: (0, 0))
        return pl.pallas_call(
            functools.partial(attend_back_kernel, heads, self.scale),
            name="attend_back",
            out_shape=(
                jax.ShapeDtypeStruct((REACH * rows, feats), BF),
                jax.ShapeDtypeStruct((REACH * rows, 2 * feats), BF),
                jax.ShapeDtypeStruct((REACH * rows, 2 * feats), F32),
                jax.ShapeDtypeStruct((REACH * rows, 2 * feats), BF),
            ),
            grid_spec=pltpu.PrefetchScalarGridSpec(
                num_scalar_prefetch=4, grid=(REACH,),
                in_specs=[tile, tile, tile, lse, kspec, kspec, kspec, qid, kid],
                out_specs=[tile, whole, whole, whole],
                scratch_shapes=[
                    pltpu.VMEM((count * rows, feats), BF),
                    pltpu.VMEM((count * rows, feats), BF),
                    pltpu.VMEM((count, feats, rows), BF),
                    pltpu.VMEM((count * rows, feats), F32),
                    pltpu.VMEM((count * rows, feats), F32),
                    pltpu.VMEM((feats, width), F32),
                ],
            ),
            cost_estimate=self.cost(5),
        )(self.qlo, self.qhi, self.lo, self.hi, q, out, grad, lse_value, *keys, self.qid, self.kid)


def layer_norm_forward(x, gain, shift):
    mean = jnp.mean(x, axis=-1, keepdims=True)
    centred = x - mean
    inverse = lax.rsqrt(jnp.mean(centred * centred, axis=-1, keepdims=True) + EPS)
    standard = centred * inverse
    return standard, inverse, standard * gain + shift


def layer_norm_backward(upstream, standard, inverse, gain):
    scaled = upstream * gain
    inner = scaled - jnp.mean(scaled, axis=-1, keepdims=True)
    return inverse * (inner - standard * jnp.mean(scaled * standard, axis=-1, keepdims=True))


def gelu_pair(pre):
    cumul = 0.5 * (1.0 + lax.erf(pre * ROOT_HALF))
    return pre * cumul, cumul + pre * INV_ROOT_TWO_PI * jnp.exp(-0.5 * pre * pre)


def to_heads(value, place):
    rows, kinds, local = value.shape
    share = local // REACH
    groups = [value[:, :, g * share : (g + 1) * share].reshape(rows, kinds * share) for g in range(REACH)]
    mine = relative(groups, place)
    mine = [mine[0]] + [swap_tok(mine[j], j) for j in range(1, REACH)]
    return jnp.concatenate(mine, axis=0)


def from_heads(value, place, kinds):
    rows, share = value.shape[0] // REACH, value.shape[1] // kinds
    parts = [value[j * rows : (j + 1) * rows] for j in range(REACH)]
    parts = [parts[0]] + [swap_tok(parts[j], j) for j in range(1, REACH)]
    groups = relative(parts, place)
    return jnp.concatenate([g.reshape(rows, kinds, share) for g in groups], axis=2)


def per_device(tokens, cotangent, image_ids, w_qkv, w_out, w_up, w_down, vectors):
    layers, block = w_qkv.shape[0], w_qkv.shape[1]
    rows, width = tokens.shape
    local, hidden = w_qkv.shape[3], w_up.shape[2]
    count, parts = lax.axis_size("tok"), lax.axis_size("tp")
    vrows = vectors.shape[1]
    part = lax.axis_index("tp")
    place = lax.axis_index("tok") % REACH

    small_cols = vectors.transpose(2, 0, 1).reshape(block, layers * vrows)
    pad = -(layers * vrows) % 128
    small_cols = jnp.pad(small_cols, ((0, 0), (0, pad)))

    def flat(w):
        return w.reshape(block, -1)

    first = gather_rows(jnp.concatenate([flat(w_qkv[0]), small_cols], axis=1))
    small = first[:, 3 * local : 3 * local + layers * vrows].T.reshape(layers, vrows, width).astype(F32)
    weights = []
    for n in range(layers):
        if n == 0:
            qkv = first[:, : 3 * local]
            rest = gather_rows(jnp.concatenate([w_out[0], w_up[0], w_down[0]], axis=1))
        else:
            rest = gather_rows(jnp.concatenate([flat(w_qkv[n]), w_out[n], w_up[n], w_down[n]], axis=1))
            qkv, rest = rest[:, : 3 * local], rest[:, 3 * local :]
        weights.append((qkv, rest[:, :local], rest[:, local : local + hidden], rest[:, local + hidden :]))

    own_ids = (image_ids + 1).reshape(1, rows)
    group = jnp.concatenate([own_ids] + [swap_tok(own_ids, j) for j in range(1, REACH)], axis=0)
    ids = jnp.concatenate([shift_tok(group, REACH), group, shift_tok(group, -REACH)], axis=0)
    attention = Attention(ids, rows, local // REACH)
    share = local // REACH

    x = tokens.astype(F32)
    saved = []
    for n in range(layers):
        qkv, out, up, down = weights[n]
        vec = small[n]
        q_bias = lax.dynamic_slice_in_dim(vec[2], part * local, local)
        v_bias = lax.dynamic_slice_in_dim(vec[3], part * local, local)
        up_bias = lax.dynamic_slice_in_dim(vec[10:].reshape(-1), part * hidden, hidden)
        bias = jnp.concatenate([q_bias, jnp.zeros_like(q_bias), v_bias])
        std1, inv1, norm1 = layer_norm_forward(x, vec[0], vec[1])
        h1 = norm1.astype(BF)
        mixed = jnp.dot(h1, qkv, preferred_element_type=F32) + bias
        mixed = mixed.astype(BF).reshape(rows, 3, local)
        together = to_heads(mixed, place)
        q = together[:, :share]
        own_keys = lax.optimization_barrier(together[:, share:])
        keys = (shift_tok(own_keys, REACH), own_keys, shift_tok(own_keys, -REACH))
        att, lse = attention.forward(q, keys)
        a = from_heads(att, place, 1).reshape(rows, local)
        branch1 = over_tp(_nt(a, out)) + vec[4]
        mid = x + vec[5] * branch1
        std2, inv2, norm2 = layer_norm_forward(mid, vec[6], vec[7])
        h2 = norm2.astype(BF)
        act, slope = gelu_pair(jnp.dot(h2, up, preferred_element_type=F32) + up_bias)
        g = act.astype(BF)
        branch2 = over_tp(_nt(g, down)) + vec[8]
        saved.append((std1, inv1, h1, q, keys, att, lse, a, branch1, std2, inv2, h2, slope, g, branch2))
        x = mid + vec[9] * branch2

    dx = cotangent.astype(F32)
    grads = [None] * layers
    vec_grads = [None] * layers

    def tn(a, b):
        return lax.dot_general(a, b, (((0,), (0,)), ((), ())), preferred_element_type=F32).astype(BF)

    def placed(piece, total):
        return lax.dynamic_update_slice_in_dim(jnp.zeros((total,), F32), piece, part * piece.shape[0], 0)

    for n in reversed(range(layers)):
        qkv, out, up, down = weights[n]
        vec = small[n]
        std1, inv1, h1, q, keys, att, lse, a, branch1, std2, inv2, h2, slope, g, branch2 = saved[n]
        ds2 = jnp.sum(dx * branch2, axis=0)
        dbranch2 = vec[9] * dx
        db2 = jnp.sum(dbranch2, axis=0)
        low2 = dbranch2.astype(BF)
        dpre = jnp.dot(low2, down, preferred_element_type=F32) * slope
        db1 = jnp.sum(dpre, axis=0)
        low_pre = dpre.astype(BF)
        dh2 = over_tp(_nt(low_pre, up))
        mlp = scatter_rows(jnp.concatenate([tn(h2, low_pre), tn(low2, g)], axis=1))
        dg2 = jnp.sum(dh2 * std2, axis=0)
        dc2 = jnp.sum(dh2, axis=0)
        dmid = dx + layer_norm_backward(dh2, std2, inv2, vec[6])
        ds1 = jnp.sum(dmid * branch1, axis=0)
        dbranch1 = vec[5] * dmid
        dbo = jnp.sum(dbranch1, axis=0)
        low1 = dbranch1.astype(BF)
        datt = jnp.dot(low1, out, preferred_element_type=F32).astype(BF)
        grad = to_heads(datt.reshape(rows, 1, local), place)
        dq, d_before, d_own, d_after = attention.backward(q, keys, att, lse, grad)
        back = shift_tok(d_before, -REACH).astype(F32) + shift_tok(d_after, REACH).astype(F32)
        dkv = (d_own + back).astype(BF)
        dmixed = from_heads(jnp.concatenate([dq, dkv], axis=1), place, 3).reshape(rows, 3 * local)
        dbq = jnp.sum(dmixed[:, :local].astype(F32), axis=0)
        dbv = jnp.sum(dmixed[:, 2 * local :].astype(F32), axis=0)
        dh1 = over_tp(_nt(dmixed, qkv))
        att_rows = scatter_rows(jnp.concatenate([tn(h1, dmixed), tn(low1, a)], axis=1))
        dg1 = jnp.sum(dh1 * std1, axis=0)
        dc1 = jnp.sum(dh1, axis=0)
        dx = dmid + layer_norm_backward(dh1, std1, inv1, vec[0])
        split = jnp.stack([placed(dbq, width), placed(dbv, width)])
        split = jnp.concatenate([split, placed(db1, parts * hidden).reshape(-1, width)], axis=0)
        split = lax.optimization_barrier(split)
        split = split + swap_tp(split)
        vec_grads[n] = jnp.concatenate(
            [jnp.stack([dg1, dc1]), split[:2], jnp.stack([dbo, ds1, dg2, dc2, db2, ds2]), split[2:]], axis=0
        )
        grads[n] = (
            att_rows[:, : 3 * local].reshape(block, 3, local),
            att_rows[:, 3 * local :],
            mlp[:, :hidden],
            mlp[:, hidden:],
        )
    vec_all = jnp.stack(vec_grads).reshape(layers * vrows, count, block).transpose(1, 0, 2)
    vec_own = scatter_small(vec_all.reshape(count, -1)).reshape(layers, vrows, block)
    half = block // parts
    vec_own = lax.dynamic_slice_in_dim(vec_own, part * half, half, 2)
    stacked = [jnp.stack([grads[n][k] for n in range(layers)]).astype(F32) for k in range(4)]
    return (x, dx, *stacked, vec_own)


def solution(mesh):
    in_specs = (
        P("tok", None),
        P("tok", None),
        P("tok"),
        P(None, "tok", None, "tp"),
        P(None, "tok", "tp"),
        P(None, "tok", "tp"),
        P(None, "tok", "tp"),
        P(None, None, "tok"),
    )
    out_specs = (
        P("tok", None),
        P("tok", None),
        P(None, "tok", None, "tp"),
        P(None, "tok", "tp"),
        P(None, "tok", "tp"),
        P(None, "tok", "tp"),
        P(None, None, ("tok", "tp")),
    )
    return jax.shard_map(per_device, mesh=mesh, in_specs=in_specs, out_specs=out_specs, check_vma=False)
```

```python
import functools
import math

import jax
import jax.numpy as jnp
from jax import lax
from jax.experimental import pallas as pl
from jax.experimental.pallas import tpu as pltpu
from jax.sharding import PartitionSpec as P

HEAD = 64
REACH = 4
EPS = 1e-06
NEG = -1e30
ROOT_HALF = 0.7071067811865476
INV_ROOT_TWO_PI = 0.3989422804014327
BF = jnp.bfloat16
F32 = jnp.float32


def swap_tok(x, mask):
    count = lax.axis_size("tok")
    return lax.ppermute(x, "tok", [(i, i ^ mask) for i in range(count)])


def swap_core(x, mask0, mask1):
    count, parts = lax.axis_size("tok"), lax.axis_size("tp")
    pairs = [
        (t * parts + c, (t ^ (mask1 if c % 2 else mask0)) * parts + c)
        for t in range(count)
        for c in range(parts)
    ]
    return lax.ppermute(x, ("tok", "tp"), pairs)


def shift_tok(x, by):
    count = lax.axis_size("tok")
    return lax.ppermute(x, "tok", [(i, i + by) for i in range(count) if 0 <= i + by < count])


def swap_tp(x):
    return lax.ppermute(x, "tp", [(0, 1), (1, 0)])


def over_tp(value):
    own = lax.optimization_barrier(value.astype(BF))
    return own.astype(F32) + swap_tp(own).astype(F32)


def gather_rows(x):
    return lax.all_gather(x, "tok", axis=0, tiled=True)


def scatter_rows(x):
    return lax.psum_scatter(x, "tok", scatter_dimension=0, tiled=True)


def scatter_small(x):
    count = lax.axis_size("tok")
    upper = count // REACH
    me = lax.axis_index("tok")
    x = jnp.take(x, jnp.arange(count) ^ me, axis=0).reshape(upper, REACH, -1)
    d0, d1, d2, d3 = (x[:, q] for q in range(REACH))
    send = lax.optimization_barrier(d3.astype(BF))
    d2 = d2 + swap_tok(send, 1).astype(F32)
    d0 = d0 + swap_tok(lax.optimization_barrier(d1.astype(BF)), 1).astype(F32)
    d0 = d0 + swap_tok(lax.optimization_barrier(d2.astype(BF)), 2).astype(F32)
    low = lax.optimization_barrier(d0.astype(BF))
    total = d0[0]
    for j in range(1, upper):
        total = total + swap_tok(low[j], REACH * j).astype(F32)
    return total


def placement():
    me = lax.axis_index("tok")
    return jnp.stack([me // REACH, me % REACH, lax.axis_index("tp") % 2]).astype(jnp.int32)


def block_of(at, q, j):
    swapped = (q & 1) * 2 + (q >> 1)
    return (at[0] ^ j) * REACH + (at[1] ^ jnp.where(at[2] == 0, q, swapped))


def link_gather(w):
    upper = lax.axis_size("tok") // REACH
    own = jnp.concatenate([w] + [swap_tok(w, REACH * j) for j in range(1, upper)], axis=0)
    first = swap_core(own, 1, 2)
    second = swap_core(own, 2, 1)
    return own, first, second, swap_core(first, 2, 1)


def link_scatter(parts):
    d0, d1, d2, d3 = parts
    upper = lax.axis_size("tok") // REACH
    last = swap_core(d3, 2, 1)
    second = swap_core(d2, 2, 1)
    d1 = (d1.astype(F32) + last.astype(F32)).astype(BF)
    first = swap_core(d1, 1, 2)
    total = d0.astype(F32) + first.astype(F32) + second.astype(F32)
    rows = total.shape[0] // upper
    low = total.astype(BF)
    result = total[:rows]
    for j in range(1, upper):
        result = result + swap_tok(low[j * rows : (j + 1) * rows], REACH * j).astype(F32)
    return result


def place_kernel(widths, at_ref, *refs):
    sources, outs = refs[:REACH], refs[REACH:]
    q = pl.program_id(0)
    for k in range(REACH):
        @pl.when(q == k)
        def _():
            start = 0
            for ref, width in zip(outs, widths):
                ref[...] = sources[k][:, start : start + width]
                start += width


def place_blocks(parts, at, widths):
    upper = lax.axis_size("tok") // REACH
    total, cols = parts[0].shape
    rows = total // upper

    def source(k):
        return pl.BlockSpec(
            (rows, cols), lambda q, j, at: (jnp.where(q == k, j, jnp.where(q > k, upper - 1, 0)), 0)
        )

    return pl.pallas_call(
        functools.partial(place_kernel, widths),
        name="place_blocks",
        out_shape=[jax.ShapeDtypeStruct((REACH * total, w), BF) for w in widths],
        grid_spec=pltpu.PrefetchScalarGridSpec(
            num_scalar_prefetch=1, grid=(REACH, upper),
            in_specs=[source(k) for k in range(REACH)],
            out_specs=[pl.BlockSpec((rows, w), lambda q, j, at: (block_of(at, q, j), 0)) for w in widths],
        ),
        cost_estimate=pl.CostEstimate(flops=0, transcendentals=0, bytes_accessed=4 * REACH * total * cols),
    )(at, *parts)


def order_matrix(at, width, block):
    upper = lax.axis_size("tok") // REACH
    col = lax.broadcasted_iota(jnp.int32, (width, width), 1)
    row = lax.broadcasted_iota(jnp.int32, (width, width), 0)
    r = col // block
    source = block_of(at, r // upper, r % upper) * block + col % block
    return (row == source).astype(BF)


def weight_grad_kernel(a1, b1, a2, b2, out_ref):
    for k, (a, b) in enumerate(((a1, b1), (a2, b2))):
        @pl.when(pl.program_id(0) == k)
        def _():
            out_ref[...] = lax.dot_general(
                a[...], b[...], (((0,), (0,)), ((), ())), preferred_element_type=F32
            ).astype(BF)


def weight_grads(a1, b1, a2, b2, tile=256):
    rows, width = a1.shape
    cols = b1.shape[1]
    steps = width // tile
    first = pl.BlockSpec((rows, tile), lambda m, i: (0, jnp.where(m == 0, i, steps - 1)))
    second = pl.BlockSpec((rows, tile), lambda m, i: (0, jnp.where(m == 0, 0, i)))
    whole = pl.BlockSpec((rows, cols), lambda m, i: (0, 0))
    return pl.pallas_call(
        weight_grad_kernel,
        name="weight_grads",
        out_shape=jax.ShapeDtypeStruct((width, 2 * cols), BF),
        grid=(2, steps),
        in_specs=[first, whole, second, whole],
        out_specs=pl.BlockSpec((tile, cols), lambda m, i: (i, m)),
        cost_estimate=pl.CostEstimate(
            flops=4 * rows * width * cols, transcendentals=0, bytes_accessed=4 * (rows + width) * cols
        ),
    )(a1, b1, a2, b2)


def relative(parts, place):
    out = []
    for j in range(REACH):
        value = parts[j ^ 3]
        for k in (2, 1, 0):
            value = jnp.where(place == k, parts[j ^ k], value)
        out.append(value)
    return out


def _stack_heads(x, heads):
    lane = lax.broadcasted_iota(jnp.int32, x.shape, 1) // HEAD
    return jnp.concatenate([jnp.where(lane == h, x, jnp.zeros_like(x)) for h in range(heads)], axis=0)


def _unstack(t, heads, width):
    rows = [t[h * HEAD : (h + 1) * HEAD, h * width : (h + 1) * width] for h in range(heads)]
    return jnp.concatenate(rows, axis=0).T


def _nt(a, b):
    return lax.dot_general(a, b, (((1,), (1,)), ((), ())), preferred_element_type=F32)


def _nn(a, b):
    return jnp.dot(a, b, preferred_element_type=F32)


def attend_kernel(heads, scale, qlo, qhi, klo, khi, q_ref, kv0, kv1, kv2, qid_ref, kid_ref,
                  o_ref, lse_ref, k_s, vt_s, acc_s, m_s, l_s):
    tq, feats = q_ref.shape
    tk = tq
    seg = kv0.shape[0] // tk
    nk = 3 * seg
    step = pl.program_id(0)

    @pl.when(step == 0)
    def _():
        for s, ref in enumerate((kv0, kv1, kv2)):
            for b in range(seg):
                at = (s * seg + b) * tk
                k_s[at : at + tk, :] = ref[b * tk : (b + 1) * tk, :feats]
                vt_s[s * seg + b] = ref[b * tk : (b + 1) * tk, feats:].astype(F32).T.astype(BF)

    q = _stack_heads(q_ref[...] * jnp.asarray(scale, BF), heads)
    qid = jnp.concatenate([qid_ref[0]] * heads, axis=1)
    m_s[...] = jnp.full_like(m_s, NEG)
    l_s[...] = jnp.zeros_like(l_s)
    acc_s[...] = jnp.zeros_like(acc_s)
    lo, hi = qlo[step], qhi[step]

    def tile(t, carry):
        @pl.when((klo[t] <= hi) & (khi[t] >= lo))
        def _():
            at = pl.multiple_of(t * tk, tk)
            s = _nt(k_s[pl.ds(at, tk), :], q)
            s = jnp.where(kid_ref[pl.ds(at, tk), :] == qid, s, NEG)
            old = m_s[...]
            new = jnp.maximum(old, jnp.max(s, axis=0, keepdims=True))
            e = jnp.exp(s - new)
            keep = jnp.exp(old - new)
            m_s[...] = new
            l_s[...] = l_s[...] * keep + jnp.sum(e, axis=0, keepdims=True)
            acc_s[...] = acc_s[...] * keep + _nn(vt_s[t], e.astype(BF))
        return carry

    lax.fori_loop(0, nk, tile, 0)
    total = l_s[...]
    o_ref[...] = _unstack(acc_s[...] / total, heads, tq).astype(BF)
    lse_ref[0] = m_s[...] + jnp.log(total)


def attend_back_kernel(heads, scale, qlo, qhi, klo, khi, q_ref, o_ref, g_ref, lse_ref, kv0, kv1, kv2,
                       qid_ref, kid_ref, dq_ref, d0_ref, d1_ref, d2_ref,
                       k_s, v_s, kt_s, dk_s, dv_s, acc_s):
    tq, feats = q_ref.shape
    tk = tq
    seg = kv0.shape[0] // tk
    nk = 3 * seg
    step = pl.program_id(0)

    @pl.when(step == 0)
    def _():
        for s, ref in enumerate((kv0, kv1, kv2)):
            for b in range(seg):
                at = (s * seg + b) * tk
                k = ref[b * tk : (b + 1) * tk, :feats]
                k_s[at : at + tk, :] = k
                v_s[at : at + tk, :] = ref[b * tk : (b + 1) * tk, feats:]
                kt_s[s * seg + b] = k.astype(F32).T.astype(BF)
        dk_s[...] = jnp.zeros_like(dk_s)
        dv_s[...] = jnp.zeros_like(dv_s)

    q = _stack_heads(q_ref[...] * jnp.asarray(scale, BF), heads)
    g = _stack_heads(g_ref[...], heads)
    prod = (o_ref[...].astype(F32) * g_ref[...].astype(F32)).T
    delta = jnp.concatenate(
        [jnp.sum(prod[h * HEAD : (h + 1) * HEAD], axis=0, keepdims=True) for h in range(heads)], axis=1
    )
    lse = lse_ref[0]
    qid = jnp.concatenate([qid_ref[0]] * heads, axis=1)
    acc_s[...] = jnp.zeros_like(acc_s)
    lo, hi = qlo[step], qhi[step]

    def tile(t, carry):
        @pl.when((klo[t] <= hi) & (khi[t] >= lo))
        def _():
            at = pl.multiple_of(t * tk, tk)
            rows = pl.ds(at, tk)
            s = _nt(k_s[rows, :], q)
            prob = jnp.exp(jnp.where(kid_ref[rows, :] == qid, s - lse, NEG))
            dv_s[rows, :] += _nn(prob.astype(BF), g)
            dp = _nt(v_s[rows, :], g)
            ds = (prob * (dp - delta)).astype(BF)
            dk_s[rows, :] += _nn(ds, q)
            acc_s[...] += _nn(kt_s[t], ds)
        return carry

    lax.fori_loop(0, nk, tile, 0)
    dq_ref[...] = (_unstack(acc_s[...], heads, tq) * scale).astype(BF)

    @pl.when(step == pl.num_programs(0) - 1)
    def _():
        for s, ref in enumerate((d0_ref, d1_ref, d2_ref)):
            at = s * seg * tk
            ref[:, :feats] = dk_s[at : at + seg * tk, :].astype(ref.dtype)
            ref[:, feats:] = dv_s[at : at + seg * tk, :].astype(ref.dtype)


class Attention:
    def __init__(self, ids, rows, feats):
        self.rows, self.feats, self.heads = rows, feats, feats // HEAD
        self.scale = 1.0 / math.sqrt(HEAD)
        self.lo, self.hi = ids[:, 0], ids[:, -1]
        own = ids[REACH : 2 * REACH]
        self.qlo, self.qhi = own[:, 0], own[:, -1]
        self.qid = own.reshape(REACH, 1, rows)
        self.kid = ids.reshape(-1, 1)

    def specs(self):
        rows, feats = self.rows, self.feats
        tile = pl.BlockSpec((rows, feats), lambda i, *_: (i, 0))
        keys = pl.BlockSpec((REACH * rows, 2 * feats), lambda i, *_: (0, 0), pipeline_mode=pl.Buffered(1))
        qid = pl.BlockSpec((1, 1, rows), lambda i, *_: (i, 0, 0))
        kid = pl.BlockSpec((3 * REACH * rows, 1), lambda i, *_: (0, 0), pipeline_mode=pl.Buffered(1))
        lse = pl.BlockSpec((1, 1, self.heads * rows), lambda i, *_: (i, 0, 0))
        return tile, keys, qid, kid, lse

    def cost(self, products):
        pairs = REACH * self.rows * 4 * self.rows * self.heads
        return pl.CostEstimate(
            flops=2 * products * pairs * self.feats, transcendentals=pairs,
            bytes_accessed=16 * REACH * self.rows * self.feats,
        )

    def forward(self, q, keys):
        tile, kspec, qid, kid, lse = self.specs()
        rows, feats, heads = self.rows, self.feats, self.heads
        width, count = heads * rows, 3 * REACH
        return pl.pallas_call(
            functools.partial(attend_kernel, heads, self.scale),
            name="attend",
            out_shape=(
                jax.ShapeDtypeStruct((REACH * rows, feats), BF),
                jax.ShapeDtypeStruct((REACH, 1, width), F32),
            ),
            grid_spec=pltpu.PrefetchScalarGridSpec(
                num_scalar_prefetch=4, grid=(REACH,),
                in_specs=[tile, kspec, kspec, kspec, qid, kid],
                out_specs=[tile, lse],
                scratch_shapes=[
                    pltpu.VMEM((count * rows, feats), BF),
                    pltpu.VMEM((count, feats, rows), BF),
                    pltpu.VMEM((feats, width), F32),
                    pltpu.VMEM((1, width), F32),
                    pltpu.VMEM((1, width), F32),
                ],
            ),
            cost_estimate=self.cost(2),
        )(self.qlo, self.qhi, self.lo, self.hi, q, *keys, self.qid, self.kid)

    def backward(self, q, keys, out, lse_value, grad):
        tile, kspec, qid, kid, lse = self.specs()
        rows, feats, heads = self.rows, self.feats, self.heads
        width, count = heads * rows, 3 * REACH
        whole = pl.BlockSpec((REACH * rows, 2 * feats), lambda i, *_: (0, 0))
        return pl.pallas_call(
            functools.partial(attend_back_kernel, heads, self.scale),
            name="attend_back",
            out_shape=(
                jax.ShapeDtypeStruct((REACH * rows, feats), BF),
                jax.ShapeDtypeStruct((REACH * rows, 2 * feats), BF),
                jax.ShapeDtypeStruct((REACH * rows, 2 * feats), F32),
                jax.ShapeDtypeStruct((REACH * rows, 2 * feats), BF),
            ),
            grid_spec=pltpu.PrefetchScalarGridSpec(
                num_scalar_prefetch=4, grid=(REACH,),
                in_specs=[tile, tile, tile, lse, kspec, kspec, kspec, qid, kid],
                out_specs=[tile, whole, whole, whole],
                scratch_shapes=[
                    pltpu.VMEM((count * rows, feats), BF),
                    pltpu.VMEM((count * rows, feats), BF),
                    pltpu.VMEM((count, feats, rows), BF),
                    pltpu.VMEM((count * rows, feats), F32),
                    pltpu.VMEM((count * rows, feats), F32),
                    pltpu.VMEM((feats, width), F32),
                ],
            ),
            cost_estimate=self.cost(5),
        )(self.qlo, self.qhi, self.lo, self.hi, q, out, grad, lse_value, *keys, self.qid, self.kid)


def layer_norm_forward(x, gain, shift):
    mean = jnp.mean(x, axis=-1, keepdims=True)
    centred = x - mean
    inverse = lax.rsqrt(jnp.mean(centred * centred, axis=-1, keepdims=True) + EPS)
    standard = centred * inverse
    return standard, inverse, standard * gain + shift


def layer_norm_backward(upstream, standard, inverse, gain):
    scaled = upstream * gain
    inner = scaled - jnp.mean(scaled, axis=-1, keepdims=True)
    return inverse * (inner - standard * jnp.mean(scaled * standard, axis=-1, keepdims=True))


def gelu_pair(pre):
    cumul = 0.5 * (1.0 + lax.erf(pre * ROOT_HALF))
    return pre * cumul, cumul + pre * INV_ROOT_TWO_PI * jnp.exp(-0.5 * pre * pre)


def to_heads(value, place, kinds):
    local = value.shape[1] // kinds
    share = local // REACH
    groups = [
        jnp.concatenate(
            [value[:, k * local + g * share : k * local + (g + 1) * share] for k in range(kinds)], axis=1
        )
        for g in range(REACH)
    ]
    mine = relative(groups, place)
    mine = [mine[0]] + [swap_tok(mine[j], j) for j in range(1, REACH)]
    return jnp.concatenate(mine, axis=0)


def from_heads(value, place, kinds):
    rows, share = value.shape[0] // REACH, value.shape[1] // kinds
    parts = [value[j * rows : (j + 1) * rows] for j in range(REACH)]
    parts = [parts[0]] + [swap_tok(parts[j], j) for j in range(1, REACH)]
    groups = relative(parts, place)
    return jnp.concatenate(
        [g[:, k * share : (k + 1) * share] for k in range(kinds) for g in groups], axis=1
    )


def per_device(tokens, cotangent, image_ids, w_qkv, w_out, w_up, w_down, vectors):
    layers, block = w_qkv.shape[0], w_qkv.shape[1]
    rows, width = tokens.shape
    local, hidden = w_qkv.shape[3], w_up.shape[2]
    count, parts = lax.axis_size("tok"), lax.axis_size("tp")
    vrows = vectors.shape[1]
    part = lax.axis_index("tp")
    place = lax.axis_index("tok") % REACH

    small_cols = vectors.transpose(2, 0, 1).reshape(block, layers * vrows)
    pad = -(layers * vrows) % 128
    small_cols = jnp.pad(small_cols, ((0, 0), (0, pad)))

    def flat(w):
        return w.reshape(block, -1)

    first = gather_rows(jnp.concatenate([flat(w_qkv[0]), small_cols], axis=1))
    small = first[:, 3 * local : 3 * local + layers * vrows].T.reshape(layers, vrows, width).astype(F32)
    at = placement()
    order = order_matrix(at, width, block)
    out_up = place_blocks(link_gather(jnp.concatenate([w_out[0], w_up[0]], axis=1)), at, (local, hidden))
    downs = place_blocks(link_gather(w_down[0]), at, (hidden,))
    weights = [(first[:, : 3 * local], *out_up, *downs)]
    for n in range(1, layers):
        rest = gather_rows(jnp.concatenate([flat(w_qkv[n]), w_out[n], w_up[n], w_down[n]], axis=1))
        qkv, rest = rest[:, : 3 * local], rest[:, 3 * local :]
        weights.append((qkv, rest[:, :local], rest[:, local : local + hidden], rest[:, local + hidden :]))

    own_ids = (image_ids + 1).reshape(1, rows)
    group = jnp.concatenate([own_ids] + [swap_tok(own_ids, j) for j in range(1, REACH)], axis=0)
    ids = jnp.concatenate([shift_tok(group, REACH), group, shift_tok(group, -REACH)], axis=0)
    attention = Attention(ids, rows, local // REACH)
    share = local // REACH

    x = tokens.astype(F32)
    saved = []
    for n in range(layers):
        qkv, out, up, down = weights[n]
        vec = small[n]
        q_bias = lax.dynamic_slice_in_dim(vec[2], part * local, local)
        v_bias = lax.dynamic_slice_in_dim(vec[3], part * local, local)
        up_bias = lax.dynamic_slice_in_dim(vec[10:].reshape(-1), part * hidden, hidden)
        bias = jnp.concatenate([q_bias, jnp.zeros_like(q_bias), v_bias])
        std1, inv1, norm1 = layer_norm_forward(x, vec[0], vec[1])
        h1 = norm1.astype(BF)
        mixed = jnp.dot(h1, qkv, preferred_element_type=F32) + bias
        together = to_heads(mixed.astype(BF), place, 3)
        q = together[:, :share]
        own_keys = lax.optimization_barrier(together[:, share:])
        keys = (shift_tok(own_keys, REACH), own_keys, shift_tok(own_keys, -REACH))
        att, lse = attention.forward(q, keys)
        a = from_heads(att, place, 1)
        branch1 = over_tp(_nt(a, out)) + vec[4]
        mid = x + vec[5] * branch1
        std2, inv2, norm2 = layer_norm_forward(mid, vec[6], vec[7])
        h2 = norm2.astype(BF)
        act, slope = gelu_pair(jnp.dot(h2, up, preferred_element_type=F32) + up_bias)
        g = act.astype(BF)
        branch2 = over_tp(_nt(g, down)) + vec[8]
        saved.append((std1, inv1, h1, q, keys, att, lse, a, branch1, std2, inv2, h2, slope, g, branch2))
        x = mid + vec[9] * branch2

    dx = cotangent.astype(F32)
    grads = [None] * layers
    vec_grads = [None] * layers

    def tn(a, b):
        return lax.dot_general(a, b, (((0,), (0,)), ((), ())), preferred_element_type=F32).astype(BF)

    def tn_parts(a, b):
        a = jnp.dot(a, order, preferred_element_type=F32).astype(BF)
        share = width // REACH
        return [tn(a[:, q * share : (q + 1) * share], b) for q in range(REACH)]

    def placed(piece, total):
        return lax.dynamic_update_slice_in_dim(jnp.zeros((total,), F32), piece, part * piece.shape[0], 0)

    for n in reversed(range(layers)):
        qkv, out, up, down = weights[n]
        vec = small[n]
        std1, inv1, h1, q, keys, att, lse, a, branch1, std2, inv2, h2, slope, g, branch2 = saved[n]
        ds2 = jnp.sum(dx * branch2, axis=0)
        dbranch2 = vec[9] * dx
        db2 = jnp.sum(dbranch2, axis=0)
        low2 = dbranch2.astype(BF)
        dpre = jnp.dot(low2, down, preferred_element_type=F32) * slope
        db1 = jnp.sum(dpre, axis=0)
        low_pre = dpre.astype(BF)
        dh2 = over_tp(_nt(low_pre, up))
        mlp_grads = weight_grads(h2, low_pre, low2, g)
        dh2, mlp_grads = lax.optimization_barrier((dh2, mlp_grads))
        mlp = scatter_rows(mlp_grads)
        dg2 = jnp.sum(dh2 * std2, axis=0)
        dc2 = jnp.sum(dh2, axis=0)
        dmid = dx + layer_norm_backward(dh2, std2, inv2, vec[6])
        ds1 = jnp.sum(dmid * branch1, axis=0)
        dbranch1 = vec[5] * dmid
        dbo = jnp.sum(dbranch1, axis=0)
        low1 = dbranch1.astype(BF)
        datt = jnp.dot(low1, out, preferred_element_type=F32).astype(BF)
        grad = to_heads(datt, place, 1)
        dq, d_before, d_own, d_after = attention.backward(q, keys, att, lse, grad)
        back = shift_tok(d_before, -REACH).astype(F32) + shift_tok(d_after, REACH).astype(F32)
        dkv = (d_own + back).astype(BF)
        dmixed = from_heads(jnp.concatenate([dq, dkv], axis=1), place, 3)
        dbq = jnp.sum(dmixed[:, :local].astype(F32), axis=0)
        dbv = jnp.sum(dmixed[:, 2 * local :].astype(F32), axis=0)
        dh1 = over_tp(_nt(dmixed, qkv))
        out_rows = link_scatter(tn_parts(low1, a))
        qkv_rows = link_scatter(tn_parts(h1, dmixed))
        dg1 = jnp.sum(dh1 * std1, axis=0)
        dc1 = jnp.sum(dh1, axis=0)
        dx = dmid + layer_norm_backward(dh1, std1, inv1, vec[0])
        split = jnp.stack([placed(dbq, width), placed(dbv, width)])
        split = jnp.concatenate([split, placed(db1, parts * hidden).reshape(-1, width)], axis=0)
        split = lax.optimization_barrier(split)
        split = split + swap_tp(split)
        vec_grads[n] = jnp.concatenate(
            [jnp.stack([dg1, dc1]), split[:2], jnp.stack([dbo, ds1, dg2, dc2, db2, ds2]), split[2:]], axis=0
        )
        grads[n] = (
            qkv_rows.reshape(block, 3, local),
            out_rows,
            mlp[:, :hidden],
            mlp[:, hidden:],
        )
    vec_all = jnp.stack(vec_grads).reshape(layers * vrows, count, block).transpose(1, 0, 2)
    vec_own = scatter_small(vec_all.reshape(count, -1)).reshape(layers, vrows, block)
    half = block // parts
    vec_own = lax.dynamic_slice_in_dim(vec_own, part * half, half, 2)
    stacked = [jnp.stack([grads[n][k] for n in range(layers)]).astype(F32) for k in range(4)]
    return (x, dx, *stacked, vec_own)


def solution(mesh):
    in_specs = (
        P("tok", None),
        P("tok", None),
        P("tok"),
        P(None, "tok", None, "tp"),
        P(None, "tok", "tp"),
        P(None, "tok", "tp"),
        P(None, "tok", "tp"),
        P(None, None, "tok"),
    )
    out_specs = (
        P("tok", None),
        P("tok", None),
        P(None, "tok", None, "tp"),
        P(None, "tok", "tp"),
        P(None, "tok", "tp"),
        P(None, "tok", "tp"),
        P(None, None, ("tok", "tp")),
    )
    return jax.shard_map(per_device, mesh=mesh, in_specs=in_specs, out_specs=out_specs, check_vma=False)
```
